32 devices in a mesh: sub: 4 (over z), row: 2 (over core), col: 4 (over y, x).
Axes of the slice: x: 2, y: 2, z: 4, core: 2. Of those that a mesh axis runs over, the one named last changes fastest.
Arguments:
- factor_cols: bfloat16 [4, 2, 2048, 4096], P('sub', None, 'col', 'row'), may hold values from -0.09375 to 0.09375
- block_pattern: int32 [4, 16, 16], P('sub'), may hold values 0 or 1
- diag_inverse: float32 [4, 4096, 2048], P('sub', ('row', 'col')), may hold values from -1 to 2
- coupling_cols: bfloat16 [4, 2, 2048, 1024], P('sub', 'row', 'col'), may hold values from -0.09375 to 0.09375
- separator_rows: int32 [4, 1024], P('sub'), may hold values from 0 to 1535, as said below
- root_inverse: float32 [1536, 1536], P('col'), may hold values from -1 to 2
- right_side: float32 [4, 4096, 128], P('sub', 'row'), may hold values from -6 to 6
- root_right: float32 [1536, 128], P('col'), may hold values from -6 to 6
Outputs:
- solution: float32 [4, 4096, 128], P('sub', ('row', 'col'))
- root_solution: float32 [1536, 128], P('col')
The draws below stay inside these ranges and needn't reach their ends.
Inputs may be any that keep to these rules, and one draw needn't show every extreme that they name: `separator_rows`: within one section the 1024 entries are distinct.
All inputs are finite; a program needn't handle non-finite values. No bound on the sum of `block_pattern` on one device may be relied on, other than what follows from the above.
Results may differ from the reference program's by a relative error of at most 0.003.
Values may be sent and summed in bfloat16 or wider, within the bound.
A program may use at most 64 MiB of HBM per device.

```python
import jax
import jax.numpy as jnp
from jax import lax

BLOCK = 256
SOURCES = 128
SEPARATOR = 1536
COUPLED = 1024
PANEL = 2048
PANELS = 2
SECTION = 4096
BLOCKS = 16
SECTIONS = 4


def inverse_blocks(key, count, order):
    noise = jnp.clip(jax.random.normal(key, (count, order, order), jnp.float32), -6.0, 6.0)
    return jnp.eye(order, dtype=jnp.float32)[None] + 0.3 * noise / jnp.sqrt(order * 1.0)


def draw_diag_inverse(key, part):
    blocks = inverse_blocks(jax.random.fold_in(key, 11), SECTIONS * PANELS, PANEL)
    return blocks.reshape(SECTIONS, SECTION, PANEL)


def draw_root_inverse(key, part):
    return inverse_blocks(jax.random.fold_in(key, 13), 1, SEPARATOR)[0]


def draw_separator_rows(key, part):

    def one_section(section_key):
        first_key, second_key = jax.random.split(section_key)
        inner = jax.random.permutation(first_key, SEPARATOR - 2)[:COUPLED - 2] + 1
        values = jnp.concatenate([jnp.array([0, SEPARATOR - 1], jnp.int32), inner.astype(jnp.int32)])
        return values[jax.random.permutation(second_key, COUPLED)]
    return jax.vmap(one_section)(jax.random.split(jax.random.fold_in(key, 17), SECTIONS))


def place_ends(values, stream_key, low, top_value):
    place = [jax.random.randint(jax.random.fold_in(stream_key, axis), (), 0, length) for axis, length in enumerate(values.shape)]
    widest = values.shape.index(max(values.shape))
    beside = place[:widest] + [(place[widest] + 1) % values.shape[widest]] + place[widest + 1:]
    return values.at[tuple(place)].set(low).at[tuple(beside)].set(top_value)


def steps_of(own_key, extent, cuts, smallest, high):
    loudness = 1.0
    for axis_at, shards_of in cuts:
        heights = jax.random.uniform(jax.random.fold_in(jax.random.fold_in(own_key, 6), axis_at), (shards_of,), jnp.float32, smallest / len(cuts), high / len(cuts))
        loudness = loudness * jnp.repeat(jnp.exp(heights), extent[axis_at] // shards_of).reshape((-1,) + (1,) * (len(extent) - 1 - axis_at))
    return loudness


def normal_values(key, dims, width, most, shards=(), kind=jnp.bfloat16):
    entries = jax.random.normal(key, dims, jnp.float32) * width
    if len(shards) > 0:
        entries = steps_of(key, dims, shards, -0.22, 0.18) * entries
    return jnp.clip(entries, min=-most, max=most).astype(kind)


def setup_inputs(seed: int = 0) -> dict:
    seeds = jax.random.split(jax.random.key(seed), 9)
    factor_cols = normal_values(seeds[0], (SECTIONS, PANELS, PANEL, SECTION), SECTION ** -0.5, 0.09375, ((0, 4), (2, 4), (3, 2)))
    block_pattern = place_ends((jax.random.randint(seeds[1], (SECTIONS, BLOCKS, BLOCKS), 0, 3) < 2).astype(jnp.int32), jax.random.fold_in(seeds[1], 1), 0, 1)
    diag_inverse = draw_diag_inverse(jax.random.fold_in(seeds[8], 71), 0)
    coupling_cols = normal_values(seeds[3], (SECTIONS, PANELS, PANEL, COUPLED), SECTION ** -0.5, 0.09375, ((0, 4), (1, 2), (2, 4)))
    separator_rows = draw_separator_rows(jax.random.fold_in(seeds[8], 71), 0)
    root_inverse = draw_root_inverse(jax.random.fold_in(seeds[8], 71), 0)
    right_side = normal_values(seeds[6], (SECTIONS, SECTION, SOURCES), 1.0, 6.0, ((0, 4), (1, 2)), jnp.float32)
    root_right = normal_values(seeds[7], (SEPARATOR, SOURCES), 1.0, 6.0, ((0, 4),), jnp.float32)
    return {"factor_cols": factor_cols, "block_pattern": block_pattern, "diag_inverse": diag_inverse, "coupling_cols": coupling_cols, "separator_rows": separator_rows, "root_inverse": root_inverse, "right_side": right_side, "root_right": root_right}


precise = lax.Precision.HIGHEST


def reference(factor_cols, block_pattern, diag_inverse, coupling_cols, separator_rows, root_inverse, right_side, root_right):
    positions = jnp.arange(SECTION)
    row_panels = positions // PANEL
    below_all = row_panels[:, None] > row_panels[None, :]
    separator_ids = jnp.arange(SEPARATOR)
    mapped_total = jnp.zeros((SEPARATOR, SOURCES), jnp.float32)
    kept = []
    for section in range(SECTIONS):
        expanded = jnp.repeat(jnp.repeat(block_pattern[section], BLOCK, axis=0), BLOCK, axis=1)
        lower_mask = jnp.where(below_all, expanded, 0).astype(jnp.bfloat16)
        masked_cols = factor_cols[section].reshape(SECTION, SECTION) * lower_mask.T
        coupled = coupling_cols[section].reshape(SECTION, COUPLED)
        solved_parts = []
        rounded_parts = []
        for current in range(PANELS):
            rows_now = slice(current * PANEL, (current + 1) * PANEL)
            panel_total = jnp.zeros((PANEL, SOURCES), jnp.float32)
            for earlier in range(current):
                cols_then = slice(earlier * PANEL, (earlier + 1) * PANEL)
                panel_total = panel_total + jnp.dot(masked_cols[cols_then, rows_now].T, rounded_parts[earlier], preferred_element_type=jnp.float32)
            solved = jnp.dot(diag_inverse[section, rows_now], right_side[section, rows_now] - panel_total, precision=precise, preferred_element_type=jnp.float32)
            solved_parts.append(solved)
            rounded_parts.append(solved.astype(jnp.bfloat16))
        rounded_all = jnp.concatenate(rounded_parts, axis=0)
        onehot = (separator_ids[:, None] == separator_rows[section][None, :]).astype(jnp.float32)
        contribution = jnp.dot(coupled.T, rounded_all, preferred_element_type=jnp.float32)
        mapped_total = mapped_total + jnp.dot(onehot, contribution, precision=precise, preferred_element_type=jnp.float32)
        kept.append((section, masked_cols, coupled, onehot, solved_parts))
    root_half = jnp.dot(root_inverse, root_right - mapped_total, precision=precise, preferred_element_type=jnp.float32)
    root_solution = jnp.dot(root_inverse.T, root_half, precision=precise, preferred_element_type=jnp.float32)
    outputs = []
    for section, masked_cols, coupled, onehot, solved_parts in kept:
        picked = jnp.dot(onehot.T, root_solution, precision=precise, preferred_element_type=jnp.float32).astype(jnp.bfloat16)
        couple_back = jnp.dot(coupled, picked, preferred_element_type=jnp.float32)
        finished = [None] * PANELS
        finished_low = [None] * PANELS
        for current in range(PANELS - 1, -1, -1):
            rows_now = slice(current * PANEL, (current + 1) * PANEL)
            panel_total = couple_back[rows_now]
            for later in range(current + 1, PANELS):
                rows_later = slice(later * PANEL, (later + 1) * PANEL)
                panel_total = panel_total + jnp.dot(masked_cols[rows_now, rows_later], finished_low[later], preferred_element_type=jnp.float32)
            value = jnp.dot(diag_inverse[section, rows_now].T, solved_parts[current] - panel_total, precision=precise, preferred_element_type=jnp.float32)
            finished[current] = value
            finished_low[current] = value.astype(jnp.bfloat16)
        outputs.append(jnp.concatenate(finished, axis=0))
    return jnp.stack(outputs), root_solution
```

```python
import functools

import jax
import jax.numpy as jnp
from jax import lax
from jax.experimental import pallas as pl
from jax.experimental.pallas import tpu as pltpu
from jax.sharding import PartitionSpec as P

BLOCK = 256
F32 = jnp.float32
BF16 = jnp.bfloat16
ROOT_TYPE = BF16


def mm(a, b):
    return lax.dot_general(a, b, (((1,), (0,)), ((), ())), preferred_element_type=F32)


def mm_nt(a, b):
    return lax.dot_general(a, b, (((1,), (1,)), ((), ())), preferred_element_type=F32)


def halves(x):
    high = x.astype(BF16)
    low = (x - high.astype(F32)).astype(BF16)
    return high, low


def paired(x):
    return jnp.concatenate(halves(x), axis=1)


def mm_paired(high, low, pair):
    both = mm(high, pair) + mm(low, pair)
    sources = pair.shape[1] // 2
    return both[:, :sources] + both[:, sources:]


def kernel(
    sizes,
    factor_hbm,
    pattern,
    inverse_hbm,
    couple_hbm,
    rows_ref,
    root_hbm,
    right_hbm,
    root_right,
    x_out,
    root_out,
    e_raw,
    m_raw,
    c_raw,
    r_raw,
    b_raw,
    e_hi,
    e_lo,
    et_hi,
    et_lo,
    m_mask,
    m_turn,
    spread,
    spread_turn,
    r_hi,
    r_lo,
    rt_hi,
    rt_lo,
    y_keep,
    y_low,
    y_first,
    mapped_snd,
    mapped_rcv,
    a_snd,
    a_rcv,
    a_all,
    s_snd,
    s_rcv,
    z_snd,
    z_rcv,
    rhs_all,
    t_snd,
    t_rcv,
    sep_low,
    root_keep,
    back_snd,
    back_rcv,
    x_all,
    give,
    take,
    load_sem,
    pair_snd,
    pair_rcv,
    col_snd,
    col_rcv,
    z_ssem,
    z_rsem,
):
    subs, cols = sizes
    sub = lax.axis_index("sub")
    row = lax.axis_index("row")
    col = lax.axis_index("col")
    width = e_raw.shape[0]
    panel = e_raw.shape[1]
    share = r_raw.shape[0]
    separator = r_raw.shape[1]

    def load(source, target, index):
        copy = pltpu.make_async_copy(source, target, load_sem.at[index])
        copy.start()
        return copy

    get_e = load(inverse_hbm.at[0], e_raw, 0)
    get_b = load(right_hbm.at[0], b_raw, 1)
    get_m = load(factor_hbm.at[0, 0], m_raw, 2)
    get_c = load(couple_hbm.at[0, 0], c_raw, 3)
    get_r = load(root_hbm, r_raw, 4)

    barrier = pltpu.get_barrier_semaphore()
    pl.semaphore_signal(barrier, inc=1, device_id={"row": 1 - row})
    for d in range(1, cols):
        pl.semaphore_signal(barrier, inc=1, device_id={"col": lax.rem(col + d, cols)})
    for d in range(1, subs):
        pl.semaphore_signal(barrier, inc=1, device_id={"sub": lax.rem(sub + d, subs)})
    pl.semaphore_wait(barrier, 1 + (cols - 1) + (subs - 1))

    def ahead(d):
        return lax.rem(col + d, cols)

    def behind(d):
        return lax.rem(col + cols - d, cols)

    def part(k, size):
        return pl.ds(pl.multiple_of(k * size, size), size)

    def to_pair(source, target, index):
        return pltpu.make_async_remote_copy(
            source, target, pair_snd.at[index], pair_rcv.at[index], device_id={"row": 1 - row}
        )

    def to_col(source, target, stage, d):
        return pltpu.make_async_remote_copy(
            source, target, col_snd.at[stage, d], col_rcv.at[stage, d], device_id={"col": ahead(d)}
        )

    def scatter(make, send, receive, stage):
        copies = []
        for d in range(1, cols):
            send[d] = make(ahead(d)).astype(send.dtype)
            copy = to_col(send.at[d], receive.at[d], stage, d)
            copy.start()
            copies.append(copy)
        return make(col), copies

    def gathered(own, receive, copies):
        for d, copy in zip(range(1, cols), copies):
            copy.wait_recv()
            own = own + receive[d].astype(F32)
        return own

    def share_out(buffer, place, stage):
        copies = []
        for d in range(1, cols):
            copy = to_col(buffer.at[place], buffer.at[place], stage, d)
            copy.start()
            copies.append(copy)
        return copies

    def finish(copies):
        for copy in copies:
            copy.wait_send()

    def split_inverse():
        for k in range(cols):
            e_hi[k], e_lo[k] = halves(e_raw[:, k * width : (k + 1) * width])

    def turn_inverse():
        for k in range(cols):
            et_hi[k], et_lo[k] = halves(e_raw[:, k * width : (k + 1) * width].T)

    def apply_inverse():
        total = jnp.zeros((width, b_raw.shape[1]), F32)
        for k in range(cols):
            pair = paired(b_raw[k * width : (k + 1) * width, :])
            total = total + mm_paired(e_hi[k], e_lo[k], pair)
        return total

    step = min(BLOCK, separator)

    def hits(first):
        at = lax.broadcasted_iota(jnp.int32, (step, rows_ref.shape[1]), 0) + first
        return jnp.where(at == rows_ref[...], 1.0, 0.0).astype(BF16)

    def make_spread():
        for first in range(0, separator, step):
            spread[first : first + step, :] = mm_nt(hits(first), c_raw[...]).astype(BF16)

    def make_spread_turn():
        for first in range(0, separator, step):
            spread_turn[:, first : first + step] = mm_nt(c_raw[...], hits(first)).astype(BF16)

    @pl.when(row == 0)
    def _():
        get_e.wait()
        get_b.wait()
        split_inverse()
        value = apply_inverse()
        y_keep[...] = value
        y_low[...] = value.astype(BF16)
        first = to_pair(y_low, y_first, 0)
        first.start()
        get_c.wait()
        make_spread()
        mapped_snd[...] = mm(spread[...], y_low[...])
        second = to_pair(mapped_snd, mapped_rcv, 1)
        second.start()
        make_spread_turn()
        turn_inverse()
        get_m.wait()
        get_r.wait()
        to_pair(sep_low, sep_low, 2).wait_recv()
        y_keep[...] = y_keep[...] - mm(spread_turn[...], sep_low[...])
        to_pair(root_keep, root_keep, 3).wait_recv()
        root_out[...] = root_keep[...]
        to_pair(give, take, 4).wait_recv()
        pair = paired(y_keep[...] - take[...])
        own, copies = scatter(
            lambda k: mm_paired(et_hi[k], et_lo[k], pair), back_snd, back_rcv, 4
        )
        x_out[0] = gathered(own, back_rcv, copies)
        finish(copies + [first, second])

    @pl.when(row != 0)
    def _():
        tall = min(width, BLOCK)
        get_m.wait()
        for at in range(0, width, tall):
            column = (col * width + at) // BLOCK
            for block in range(panel // BLOCK):
                present = pattern[0, panel // BLOCK + block, column].astype(F32)
                ends = slice(block * BLOCK, (block + 1) * BLOCK)
                kept = m_raw[at : at + tall, ends].astype(F32) * present
                m_raw[at : at + tall, ends] = kept.astype(BF16)
        for k in range(cols):
            piece = m_raw[:, k * width : (k + 1) * width]
            m_mask[k] = piece
            m_turn[k] = piece.astype(F32).T.astype(BF16)
        to_pair(y_low, y_first, 0).wait_recv()
        low = y_first[...]
        own, sends_a = scatter(lambda k: mm(m_turn[k], low), a_snd, a_rcv, 0)
        get_e.wait()
        get_b.wait()
        split_inverse()
        started = apply_inverse()
        own = gathered(own, a_rcv, sends_a)
        a_all[col] = own.astype(BF16)
        sends_b = share_out(a_all, col, 1)
        get_c.wait()
        make_spread()
        value = started
        for d in range(cols):
            k = behind(d)
            if d > 0:
                sends_b[d - 1].wait_recv()
            value = value - (mm(e_hi[k], a_all[k]) + mm(e_lo[k], a_all[k]))
        y_keep[...] = value
        y_low[...] = value.astype(BF16)
        to_pair(mapped_snd, mapped_rcv, 1).wait_recv()
        own_low = y_low[...]
        own, sends_c = scatter(
            lambda k: mm(spread[part(k, share), :], own_low) + mapped_rcv[part(k, share), :],
            s_snd,
            s_rcv,
            2,
        )
        get_r.wait()
        r_hi[...], r_lo[...] = halves(r_raw[...])
        for first in range(0, separator, step):
            ends = slice(first, first + step)
            rt_hi[ends, :], rt_lo[ends, :] = halves(r_raw[:, ends].T)
        own = gathered(own, s_rcv, sends_c)
        z_snd[...] = own.astype(z_snd.dtype)
        sends_z = []
        for d in range(1, subs):
            copy = pltpu.make_async_remote_copy(
                z_snd,
                z_rcv.at[d],
                z_ssem.at[d],
                z_rsem.at[d],
                device_id={"sub": lax.rem(sub + d, subs)},
            )
            copy.start()
            sends_z.append(copy)
        make_spread_turn()
        turn_inverse()
        for d, copy in zip(range(1, subs), sends_z):
            copy.wait_recv()
            own = own + z_rcv[d].astype(F32)
        rhs_all[part(col, share), :] = (root_right[...] - own).astype(rhs_all.dtype)
        sends_d = share_out(rhs_all, part(col, share), 3)
        for copy in sends_d:
            copy.wait_recv()
        if rhs_all.dtype == BF16:
            half = mm(r_hi[...], rhs_all[...]) + mm(r_lo[...], rhs_all[...])
        else:
            half = mm_paired(r_hi[...], r_lo[...], paired(rhs_all[...]))
        pair_r = paired(half)
        own, sends_e = scatter(
            lambda k: mm_paired(rt_hi[part(k, share), :], rt_lo[part(k, share), :], pair_r),
            t_snd,
            t_rcv,
            5,
        )
        own = gathered(own, t_rcv, sends_e)
        sep_low[part(col, share), :] = own.astype(BF16)
        sends_f = share_out(sep_low, part(col, share), 6)
        root_out[...] = own
        root_keep[...] = own
        third = to_pair(root_keep, root_keep, 3)
        third.start()
        for copy in sends_f:
            copy.wait_recv()
        fourth = to_pair(sep_low, sep_low, 2)
        fourth.start()
        pair = paired(y_keep[...] - mm(spread_turn[...], sep_low[...]))
        own, sends_g = scatter(
            lambda k: mm_paired(et_hi[k], et_lo[k], pair), back_snd, back_rcv, 4
        )
        own = gathered(own, back_rcv, sends_g)
        x_all[col] = own.astype(BF16)
        sends_h = share_out(x_all, col, 7)
        x_out[0] = own
        total = jnp.zeros((width, own.shape[1]), F32)
        for d in range(cols):
            k = behind(d)
            if d > 0:
                sends_h[d - 1].wait_recv()
            total = total + mm(m_mask[k], x_all[k])
        give[...] = total
        fifth = to_pair(give, take, 4)
        fifth.start()
        finish(sends_a + sends_b + sends_c + sends_z + sends_d + sends_e + sends_f + sends_g)
        finish(sends_h + [third, fourth, fifth])


def shards(
    sizes,
    factor_cols,
    block_pattern,
    diag_inverse,
    coupling_cols,
    separator_rows,
    root_inverse,
    right_side,
    root_right,
):
    subs, cols = sizes
    width, panel = diag_inverse.shape[1:]
    share, separator = root_inverse.shape
    sources = right_side.shape[2]
    coupled = coupling_cols.shape[3]
    hbm = pl.BlockSpec(memory_space=pl.ANY)
    vmem = pl.BlockSpec(memory_space=pltpu.VMEM)
    smem = pl.BlockSpec(memory_space=pltpu.SMEM)
    V = pltpu.VMEM
    tile = (cols, width, width)
    scratch = [
        V((width, panel), F32),
        V((width, panel), BF16),
        V((width, coupled), BF16),
        V((share, separator), F32),
        V((panel, sources), F32),
        V(tile, BF16),
        V(tile, BF16),
        V(tile, BF16),
        V(tile, BF16),
        V(tile, BF16),
        V(tile, BF16),
        V((separator, width), BF16),
        V((width, separator), BF16),
        V((share, separator), BF16),
        V((share, separator), BF16),
        V((separator, share), BF16),
        V((separator, share), BF16),
        V((width, sources), F32),
        V((width, sources), BF16),
        V((width, sources), BF16),
        V((separator, sources), F32),
        V((separator, sources), F32),
        V((cols, width, sources), BF16),
        V((cols, width, sources), BF16),
        V((cols, width, sources), BF16),
        V((cols, share, sources), BF16),
        V((cols, share, sources), BF16),
        V((share, sources), BF16),
        V((subs, share, sources), BF16),
        V((separator, sources), ROOT_TYPE),
        V((cols, share, sources), BF16),
        V((cols, share, sources), BF16),
        V((separator, sources), BF16),
        V((share, sources), F32),
        V((cols, width, sources), BF16),
        V((cols, width, sources), BF16),
        V((cols, width, sources), BF16),
        V((width, sources), F32),
        V((width, sources), F32),
        pltpu.SemaphoreType.DMA((5,)),
        pltpu.SemaphoreType.DMA((5,)),
        pltpu.SemaphoreType.DMA((5,)),
        pltpu.SemaphoreType.DMA((8, cols)),
        pltpu.SemaphoreType.DMA((8, cols)),
        pltpu.SemaphoreType.DMA((subs,)),
        pltpu.SemaphoreType.DMA((subs,)),
    ]
    return pl.pallas_call(
        functools.partial(kernel, sizes),
        out_shape=(
            jax.ShapeDtypeStruct((1, width, sources), F32),
            jax.ShapeDtypeStruct((share, sources), F32),
        ),
        in_specs=[hbm, smem, hbm, hbm, vmem, hbm, hbm, vmem],
        out_specs=(vmem, vmem),
        scratch_shapes=scratch,
        compiler_params=pltpu.CompilerParams(
            collective_id=0, has_side_effects=True, vmem_limit_bytes=60 * 1024 * 1024
        ),
        name="tree_solve",
    )(
        factor_cols,
        block_pattern,
        diag_inverse,
        coupling_cols,
        separator_rows,
        root_inverse,
        right_side,
        root_right,
    )


def solution(mesh):
    sizes = (mesh.shape["sub"], mesh.shape["col"])
    return jax.shard_map(
        functools.partial(shards, sizes),
        mesh=mesh,
        in_specs=(
            P("sub", None, "col", "row"),
            P("sub", None, None),
            P("sub", ("row", "col"), None),
            P("sub", "row", "col", None),
            P("sub", None),
            P("col", None),
            P("sub", "row", None),
            P("col", None),
        ),
        out_specs=(P("sub", ("row", "col"), None), P("col", None)),
        check_vma=False,
    )
```

```python
import functools

import jax
import jax.numpy as jnp
from jax import lax
from jax.experimental import pallas as pl
from jax.experimental.pallas import tpu as pltpu
from jax.sharding import PartitionSpec as P

BLOCK = 256
F32 = jnp.float32
BF16 = jnp.bfloat16
PIECES = 2


def mm(a, b):
    return lax.dot_general(a, b, (((1,), (0,)), ((), ())), preferred_element_type=F32)


def mm_nt(a, b):
    return lax.dot_general(a, b, (((1,), (1,)), ((), ())), preferred_element_type=F32)


def halves(x):
    high = x.astype(BF16)
    low = (x - high.astype(F32)).astype(BF16)
    return high, low


def paired(x):
    return jnp.concatenate(halves(x), axis=1)


def mm_paired(high, low, pair):
    both = mm(high, pair) + mm(low, pair)
    sources = pair.shape[1] // 2
    return both[:, :sources] + both[:, sources:]


def kernel(
    sizes,
    factor_hbm,
    pattern,
    inverse_hbm,
    couple_hbm,
    rows_ref,
    root_hbm,
    right_hbm,
    root_right,
    x_out,
    root_out,
    e_raw,
    m_raw,
    c_raw,
    r_raw,
    b_raw,
    e_hi,
    e_lo,
    et_hi,
    et_lo,
    m_mask,
    m_turn,
    spread,
    spread_turn,
    r_hi,
    r_lo,
    rt_hi,
    rt_lo,
    y_keep,
    y_low,
    y_first,
    mapped_snd,
    mapped_rcv,
    a_snd,
    a_rcv,
    a_all,
    s_snd,
    s_rcv,
    z_snd,
    z_rcv,
    rhs_hi,
    rhs_lo,
    t_snd,
    t_rcv,
    sep_low,
    root_keep,
    back_snd,
    back_rcv,
    x_all,
    give,
    take,
    load_sem,
    pair_snd,
    pair_rcv,
    col_snd,
    col_rcv,
    z_ssem,
    z_rsem,
):
    subs, cols = sizes
    sub = lax.axis_index("sub")
    row = lax.axis_index("row")
    col = lax.axis_index("col")
    width = e_raw.shape[0]
    panel = e_raw.shape[1]
    share = r_raw.shape[0]
    separator = r_raw.shape[1]

    def load(source, target, index):
        return pltpu.make_async_copy(source, target, load_sem.at[index])

    get_b = load(right_hbm.at[0], b_raw, 0)
    get_m = load(factor_hbm.at[0, 0], m_raw, 1)
    get_c = load(couple_hbm.at[0, 0], c_raw, 2)
    get_r = load(root_hbm, r_raw, 3)
    get_e = []
    for k in range(cols):
        ends = pl.ds(k * width, width)
        get_e.append(load(inverse_hbm.at[0, :, ends], e_raw.at[:, ends], 4 + k))

    @pl.when(row == 0)
    def _():
        for copy in [get_b] + get_e + [get_c]:
            copy.start()

    @pl.when(row != 0)
    def _():
        for copy in [get_m] + get_e + [get_b, get_c, get_r]:
            copy.start()

    barrier = pltpu.get_barrier_semaphore()
    pl.semaphore_signal(barrier, inc=1, device_id={"row": 1 - row})
    for d in range(1, cols):
        pl.semaphore_signal(barrier, inc=1, device_id={"col": lax.rem(col + d, cols)})
    for d in range(1, subs):
        pl.semaphore_signal(barrier, inc=1, device_id={"sub": lax.rem(sub + d, subs)})

    def ahead(d):
        return lax.rem(col + d, cols)

    def behind(d):
        return lax.rem(col + cols - d, cols)

    def part(k, size):
        return pl.ds(pl.multiple_of(k * size, size), size)

    def to_pair(source, target, index):
        return pltpu.make_async_remote_copy(
            source, target, pair_snd.at[index], pair_rcv.at[index], device_id={"row": 1 - row}
        )

    def to_col(source, target, stage, d):
        return pltpu.make_async_remote_copy(
            source, target, col_snd.at[stage, d], col_rcv.at[stage, d], device_id={"col": ahead(d)}
        )

    def rows_of(piece, size):
        return pl.ds(piece * (size // PIECES), size // PIECES)

    def piece_of(k, piece, size):
        extent = size // PIECES
        return pl.ds(pl.multiple_of(k * size + piece * extent, extent), extent)

    def scatter(make, send, receive, stage):
        size = send.shape[1]
        own, copies = [], []
        for piece in range(PIECES):
            rows = rows_of(piece, size)
            sent = []
            for d in range(1, cols):
                send[d, rows, :] = make(ahead(d), piece).astype(send.dtype)
                copy = to_col(
                    send.at[d, rows], receive.at[d, rows], stage * PIECES + piece, d
                )
                copy.start()
                sent.append(copy)
            own.append(make(col, piece))
            copies.append(sent)
        return own, copies

    def gathered(own, receive, copies, piece):
        total = own[piece]
        rows = rows_of(piece, receive.shape[1])
        for d, copy in zip(range(1, cols), copies[piece]):
            copy.wait_recv()
            total = total + receive[d, rows, :].astype(F32)
        return total

    def share_out(target, slot):
        copies = []
        for d in range(1, cols):
            copy = to_col(target, target, slot, d)
            copy.start()
            copies.append(copy)
        return copies

    def finish(copies):
        for copy in copies:
            if isinstance(copy, list):
                finish(copy)
            else:
                copy.wait_send()

    def apply_inverse():
        get_b.wait()
        total = jnp.zeros((width, b_raw.shape[1]), F32)
        for k in range(cols):
            get_e[k].wait()
            high, low = halves(e_raw[:, k * width : (k + 1) * width])
            e_hi[k] = high
            e_lo[k] = low
            pair = paired(b_raw[k * width : (k + 1) * width, :])
            total = total + mm_paired(high, low, pair)
        return total

    def turn_inverse():
        for k in range(cols):
            et_hi[k], et_lo[k] = halves(e_raw[:, k * width : (k + 1) * width].T)

    step = min(BLOCK, separator)

    def hits(first):
        at = lax.broadcasted_iota(jnp.int32, (step, rows_ref.shape[1]), 0) + first
        return jnp.where(at == rows_ref[...], 1.0, 0.0).astype(BF16)

    def make_spread():
        for first in range(0, separator, step):
            spread[first : first + step, :] = mm_nt(hits(first), c_raw[...]).astype(BF16)

    def make_spread_turn():
        for first in range(0, separator, step):
            spread_turn[:, first : first + step] = mm_nt(c_raw[...], hits(first)).astype(BF16)

    @pl.when(row == 0)
    def _():
        value = apply_inverse()
        y_keep[...] = value
        y_low[...] = value.astype(BF16)

    @pl.when(row != 0)
    def _():
        tall = min(width, BLOCK)
        get_m.wait()
        for at in range(0, width, tall):
            column = (col * width + at) // BLOCK
            for block in range(panel // BLOCK):
                present = pattern[0, panel // BLOCK + block, column].astype(F32)
                ends = slice(block * BLOCK, (block + 1) * BLOCK)
                kept = m_raw[at : at + tall, ends].astype(F32) * present
                m_raw[at : at + tall, ends] = kept.astype(BF16)
        for k in range(cols):
            piece = m_raw[:, k * width : (k + 1) * width]
            m_mask[k] = piece
            m_turn[k] = piece.astype(F32).T.astype(BF16)

    pl.semaphore_wait(barrier, 1 + (cols - 1) + (subs - 1))

    def turned(pair):
        def make(k, piece):
            rows = rows_of(piece, width)
            return mm_paired(et_hi[k, rows, :], et_lo[k, rows, :], pair)

        return make

    @pl.when(row == 0)
    def _():
        first = to_pair(y_low, y_first, 0)
        first.start()
        get_c.wait()
        make_spread()
        mapped_snd[...] = mm(spread[...], y_low[...])
        second = to_pair(mapped_snd, mapped_rcv, 1)
        second.start()
        make_spread_turn()
        turn_inverse()
        to_pair(sep_low, sep_low, 2).wait_recv()
        y_keep[...] = y_keep[...] - mm(spread_turn[...], sep_low[...])
        to_pair(root_keep, root_keep, 3).wait_recv()
        root_out[...] = root_keep[...]
        to_pair(give, take, 4).wait_recv()
        pair = paired(y_keep[...] - take[...])
        own, copies = scatter(turned(pair), back_snd, back_rcv, 7)
        for piece in range(PIECES):
            x_out[0, rows_of(piece, width), :] = gathered(own, back_rcv, copies, piece)
        finish(copies + [first, second])

    @pl.when(row != 0)
    def _():
        to_pair(y_low, y_first, 0).wait_recv()
        low = y_first[...]
        own, sends_a = scatter(
            lambda k, piece: mm(m_turn[k, rows_of(piece, width), :], low), a_snd, a_rcv, 0
        )
        started = apply_inverse()
        sends_b = []
        for piece in range(PIECES):
            rows = rows_of(piece, width)
            a_all[col, rows, :] = gathered(own, a_rcv, sends_a, piece).astype(BF16)
            sends_b.append(share_out(a_all.at[col, rows], PIECES + piece))
        get_c.wait()
        make_spread()
        value = started
        for d in range(cols):
            k = behind(d)
            if d > 0:
                for piece in range(PIECES):
                    sends_b[piece][d - 1].wait_recv()
            value = value - (mm(e_hi[k], a_all[k]) + mm(e_lo[k], a_all[k]))
        y_keep[...] = value
        own_low = value.astype(BF16)
        to_pair(mapped_snd, mapped_rcv, 1).wait_recv()

        def separator_rows(k, piece):
            rows = piece_of(k, piece, share)
            return mm(spread[rows, :], own_low) + mapped_rcv[rows, :]

        own, sends_c = scatter(separator_rows, s_snd, s_rcv, 2)
        get_r.wait()
        r_hi[...], r_lo[...] = halves(r_raw[...])
        for first in range(0, separator, step):
            ends = slice(first, first + step)
            rt_hi[ends, :], rt_lo[ends, :] = halves(r_raw[:, ends].T)
        sends_z = []
        for piece in range(PIECES):
            rows = rows_of(piece, share)
            own[piece] = gathered(own, s_rcv, sends_c, piece)
            z_snd[rows, :] = own[piece].astype(BF16)
            sent = []
            for d in range(1, subs):
                copy = pltpu.make_async_remote_copy(
                    z_snd.at[rows],
                    z_rcv.at[d, rows],
                    z_ssem.at[piece, d],
                    z_rsem.at[piece, d],
                    device_id={"sub": lax.rem(sub + d, subs)},
                )
                copy.start()
                sent.append(copy)
            sends_z.append(sent)
        make_spread_turn()
        turn_inverse()
        sends_d = []
        for piece in range(PIECES):
            rows = rows_of(piece, share)
            total = own[piece]
            for d, copy in zip(range(1, subs), sends_z[piece]):
                copy.wait_recv()
                total = total + z_rcv[d, rows, :].astype(F32)
            high, low = halves(root_right[rows, :] - total)
            place = piece_of(col, piece, share)
            rhs_hi[place, :] = high
            rhs_lo[place, :] = low
            sends_d.append(share_out(rhs_hi.at[place], 3 * PIECES + piece))
        rest = share_out(rhs_lo.at[part(col, share)], 4 * PIECES)
        for sent in sends_d:
            for copy in sent:
                copy.wait_recv()
        half = mm(r_hi[...], rhs_hi[...]) + mm(r_lo[...], rhs_hi[...])
        for copy in rest:
            copy.wait_recv()
        pair_r = paired(half + mm(r_hi[...], rhs_lo[...]))

        def root_rows(k, piece):
            rows = piece_of(k, piece, share)
            return mm_paired(rt_hi[rows, :], rt_lo[rows, :], pair_r)

        own, sends_e = scatter(root_rows, t_snd, t_rcv, 5)
        sends_f = []
        for piece in range(PIECES):
            total = gathered(own, t_rcv, sends_e, piece)
            place = piece_of(col, piece, share)
            sep_low[place, :] = total.astype(BF16)
            sends_f.append(share_out(sep_low.at[place], 6 * PIECES + piece))
            root_out[rows_of(piece, share), :] = total
            root_keep[rows_of(piece, share), :] = total
        third = to_pair(root_keep, root_keep, 3)
        third.start()
        for sent in sends_f:
            for copy in sent:
                copy.wait_recv()
        fourth = to_pair(sep_low, sep_low, 2)
        fourth.start()
        pair = paired(y_keep[...] - mm(spread_turn[...], sep_low[...]))
        own, sends_g = scatter(turned(pair), back_snd, back_rcv, 7)
        sends_h = []
        for piece in range(PIECES):
            rows = rows_of(piece, width)
            total = gathered(own, back_rcv, sends_g, piece)
            x_all[col, rows, :] = total.astype(BF16)
            sends_h.append(share_out(x_all.at[col, rows], 8 * PIECES + piece))
            x_out[0, rows, :] = total
        total = jnp.zeros(give.shape, F32)
        for d in range(cols):
            k = behind(d)
            if d > 0:
                for piece in range(PIECES):
                    sends_h[piece][d - 1].wait_recv()
            total = total + mm(m_mask[k], x_all[k])
        give[...] = total
        fifth = to_pair(give, take, 4)
        fifth.start()
        finish([sends_a, sends_b, sends_c, sends_z, sends_d, rest, sends_e, sends_f])
        finish([sends_g, sends_h, third, fourth, fifth])


def shards(
    sizes,
    factor_cols,
    block_pattern,
    diag_inverse,
    coupling_cols,
    separator_rows,
    root_inverse,
    right_side,
    root_right,
):
    subs, cols = sizes
    width, panel = diag_inverse.shape[1:]
    share, separator = root_inverse.shape
    sources = right_side.shape[2]
    coupled = coupling_cols.shape[3]
    hbm = pl.BlockSpec(memory_space=pl.ANY)
    vmem = pl.BlockSpec(memory_space=pltpu.VMEM)
    smem = pl.BlockSpec(memory_space=pltpu.SMEM)
    V = pltpu.VMEM
    tile = (cols, width, width)
    scratch = [
        V((width, panel), F32),
        V((width, panel), BF16),
        V((width, coupled), BF16),
        V((share, separator), F32),
        V((panel, sources), F32),
        V(tile, BF16),
        V(tile, BF16),
        V(tile, BF16),
        V(tile, BF16),
        V(tile, BF16),
        V(tile, BF16),
        V((separator, width), BF16),
        V((width, separator), BF16),
        V((share, separator), BF16),
        V((share, separator), BF16),
        V((separator, share), BF16),
        V((separator, share), BF16),
        V((width, sources), F32),
        V((width, sources), BF16),
        V((width, sources), BF16),
        V((separator, sources), F32),
        V((separator, sources), F32),
        V((cols, width, sources), BF16),
        V((cols, width, sources), BF16),
        V((cols, width, sources), BF16),
        V((cols, share, sources), BF16),
        V((cols, share, sources), BF16),
        V((share, sources), BF16),
        V((subs, share, sources), BF16),
        V((separator, sources), BF16),
        V((separator, sources), BF16),
        V((cols, share, sources), BF16),
        V((cols, share, sources), BF16),
        V((separator, sources), BF16),
        V((share, sources), F32),
        V((cols, width, sources), BF16),
        V((cols, width, sources), BF16),
        V((cols, width, sources), BF16),
        V((width, sources), F32),
        V((width, sources), F32),
        pltpu.SemaphoreType.DMA((4 + cols,)),
        pltpu.SemaphoreType.DMA((5,)),
        pltpu.SemaphoreType.DMA((5,)),
        pltpu.SemaphoreType.DMA((10 * PIECES, cols)),
        pltpu.SemaphoreType.DMA((10 * PIECES, cols)),
        pltpu.SemaphoreType.DMA((PIECES, subs)),
        pltpu.SemaphoreType.DMA((PIECES, subs)),
    ]
    return pl.pallas_call(
        functools.partial(kernel, sizes),
        out_shape=(
            jax.ShapeDtypeStruct((1, width, sources), F32),
            jax.ShapeDtypeStruct((share, sources), F32),
        ),
        in_specs=[hbm, smem, hbm, hbm, vmem, hbm, hbm, vmem],
        out_specs=(vmem, vmem),
        scratch_shapes=scratch,
        compiler_params=pltpu.CompilerParams(
            collective_id=0, has_side_effects=True, vmem_limit_bytes=60 * 1024 * 1024
        ),
        name="tree_solve",
    )(
        factor_cols,
        block_pattern,
        diag_inverse,
        coupling_cols,
        separator_rows,
        root_inverse,
        right_side,
        root_right,
    )


def solution(mesh):
    sizes = (mesh.shape["sub"], mesh.shape["col"])
    return jax.shard_map(
        functools.partial(shards, sizes),
        mesh=mesh,
        in_specs=(
            P("sub", None, "col", "row"),
            P("sub", None, None),
            P("sub", ("row", "col"), None),
            P("sub", "row", "col", None),
            P("sub", None),
            P("col", None),
            P("sub", "row", None),
            P("col", None),
        ),
        out_specs=(P("sub", ("row", "col"), None), P("col", None)),
        check_vma=False,
    )
```

```python
import functools

import jax
import jax.numpy as jnp
from jax import lax
from jax.experimental import pallas as pl
from jax.experimental.pallas import tpu as pltpu
from jax.sharding import PartitionSpec as P

BLOCK = 256
F32 = jnp.float32
BF16 = jnp.bfloat16
PIECES = 2


def mm(a, b):
    return lax.dot_general(a, b, (((1,), (0,)), ((), ())), preferred_element_type=F32)


def mm_nt(a, b):
    return lax.dot_general(a, b, (((1,), (1,)), ((), ())), preferred_element_type=F32)


def halves(x):
    high = x.astype(BF16)
    low = (x - high.astype(F32)).astype(BF16)
    return high, low


def paired(x):
    return jnp.concatenate(halves(x), axis=1)


def mm_paired(high, low, pair):
    both = mm(high, pair) + mm(low, pair)
    sources = pair.shape[1] // 2
    return both[:, :sources] + both[:, sources:]


def kernel(
    sizes,
    factor_hbm,
    pattern_hbm,
    inverse_hbm,
    couple_hbm,
    rows_hbm,
    root_hbm,
    right_hbm,
    root_right_hbm,
    x_out,
    root_out,
    pattern,
    rows_ref,
    root_right,
    e_raw,
    m_raw,
    c_raw,
    r_raw,
    b_raw,
    e_hi,
    e_lo,
    et_hi,
    et_lo,
    m_mask,
    m_turn,
    spread,
    spread_turn,
    r_hi,
    r_lo,
    rt_hi,
    rt_lo,
    y_keep,
    y_low,
    y_first,
    mapped_snd,
    mapped_rcv,
    a_snd,
    a_rcv,
    a_all,
    s_snd,
    s_rcv,
    z_snd,
    z_rcv,
    rhs_hi,
    rhs_lo,
    t_snd,
    t_rcv,
    sep_low,
    root_keep,
    back_snd,
    back_rcv,
    x_all,
    give,
    take,
    load_sem,
    pair_snd,
    pair_rcv,
    col_snd,
    col_rcv,
    z_ssem,
    z_rsem,
):
    subs, cols = sizes
    sub = lax.axis_index("sub")
    row = lax.axis_index("row")
    col = lax.axis_index("col")
    width = e_raw.shape[0]
    panel = e_raw.shape[1]
    share = r_raw.shape[0]
    separator = r_raw.shape[1]

    def load(source, target, index):
        return pltpu.make_async_copy(source, target, load_sem.at[index])

    get_b = load(right_hbm.at[0], b_raw, 0)
    get_m = load(factor_hbm.at[0, 0], m_raw, 1)
    get_c = load(couple_hbm.at[0, 0], c_raw, 2)
    get_r = load(root_hbm, r_raw, 3)
    get_p = load(pattern_hbm, pattern, 4 + cols)
    get_s = load(rows_hbm, rows_ref, 5 + cols)
    get_t = load(root_right_hbm, root_right, 6 + cols)
    get_e = []
    for k in range(cols):
        ends = pl.ds(k * width, width)
        get_e.append(load(inverse_hbm.at[0, :, ends], e_raw.at[:, ends], 4 + k))

    @pl.when(row == 0)
    def _():
        for copy in [get_b] + get_e + [get_c, get_s]:
            copy.start()

    @pl.when(row != 0)
    def _():
        for copy in [get_p, get_m] + get_e + [get_b, get_c, get_s, get_r, get_t]:
            copy.start()

    barrier = pltpu.get_barrier_semaphore()
    pl.semaphore_signal(barrier, inc=1, device_id={"row": 1 - row})
    for d in range(1, cols):
        pl.semaphore_signal(barrier, inc=1, device_id={"col": lax.rem(col + d, cols)})
    for d in range(1, subs):
        pl.semaphore_signal(barrier, inc=1, device_id={"sub": lax.rem(sub + d, subs)})

    def partner(place, d):
        bit = 1
        while bit <= d:
            if d & bit:
                place = place + bit * (1 - 2 * (place // bit % 2))
            bit *= 2
        return place

    def other(d):
        return partner(col, d)

    order = tuple(range(cols - 1, 0, -1))
    arrival = (0,) + tuple(range(cols // 2, cols - 1)) + tuple(range(1, cols // 2)) + (cols - 1,)

    def part(k, size):
        return pl.ds(pl.multiple_of(k * size, size), size)

    def to_pair(source, target, index):
        return pltpu.make_async_remote_copy(
            source, target, pair_snd.at[index], pair_rcv.at[index], device_id={"row": 1 - row}
        )

    def to_col(source, target, stage, d):
        return pltpu.make_async_remote_copy(
            source, target, col_snd.at[stage, d], col_rcv.at[stage, d], device_id={"col": other(d)}
        )

    def rows_of(piece, size):
        return pl.ds(piece * (size // PIECES), size // PIECES)

    def piece_of(k, piece, size):
        extent = size // PIECES
        return pl.ds(pl.multiple_of(k * size + piece * extent, extent), extent)

    def scatter(make, send, receive, stage):
        size = send.shape[1]
        own, copies = [], []
        for piece in range(PIECES):
            rows = rows_of(piece, size)
            sent = []
            for d in order:
                send[d, rows, :] = make(other(d), piece).astype(send.dtype)
                copy = to_col(
                    send.at[d, rows], receive.at[d, rows], stage * PIECES + piece, d
                )
                copy.start()
                sent.append(copy)
            own.append(make(col, piece))
            copies.append(sent)
        return own, copies

    def gathered(own, receive, copies, piece):
        total = own[piece]
        rows = rows_of(piece, receive.shape[1])
        for d, copy in zip(order, copies[piece]):
            copy.wait_recv()
            total = total + receive[d, rows, :].astype(F32)
        return total

    def share_out(target, slot):
        copies = []
        for d in order:
            copy = to_col(target, target, slot, d)
            copy.start()
            copies.append(copy)
        return copies

    def finish(copies):
        for copy in copies:
            if isinstance(copy, list):
                finish(copy)
            else:
                copy.wait_send()

    def apply_inverse():
        get_b.wait()
        total = jnp.zeros((width, b_raw.shape[1]), F32)
        for k in range(cols):
            get_e[k].wait()
            high, low = halves(e_raw[:, k * width : (k + 1) * width])
            e_hi[k] = high
            e_lo[k] = low
            pair = paired(b_raw[k * width : (k + 1) * width, :])
            total = total + mm_paired(high, low, pair)
        return total

    def turn_inverse():
        for k in range(cols):
            et_hi[k], et_lo[k] = halves(e_raw[:, k * width : (k + 1) * width].T)

    step = min(BLOCK, separator)

    def hits(first):
        at = lax.broadcasted_iota(jnp.int32, (step, rows_ref.shape[1]), 0) + first
        return jnp.where(at == rows_ref[...], 1.0, 0.0).astype(BF16)

    def make_spread():
        for first in range(0, separator, step):
            spread[first : first + step, :] = mm_nt(hits(first), c_raw[...]).astype(BF16)

    def make_spread_turn():
        for first in range(0, separator, step):
            spread_turn[:, first : first + step] = mm_nt(c_raw[...], hits(first)).astype(BF16)

    @pl.when(row == 0)
    def _():
        value = apply_inverse()
        y_keep[...] = value
        y_low[...] = value.astype(BF16)

    @pl.when(row != 0)
    def _():
        tall = min(width, BLOCK)
        get_p.wait()
        get_m.wait()
        for at in range(0, width, tall):
            column = (col * width + at) // BLOCK
            for block in range(panel // BLOCK):
                present = pattern[0, panel // BLOCK + block, column].astype(F32)
                ends = slice(block * BLOCK, (block + 1) * BLOCK)
                kept = m_raw[at : at + tall, ends].astype(F32) * present
                m_raw[at : at + tall, ends] = kept.astype(BF16)
        for k in range(cols):
            piece = m_raw[:, k * width : (k + 1) * width]
            m_mask[k] = piece
            m_turn[k] = piece.astype(F32).T.astype(BF16)

    pl.semaphore_wait(barrier, 1 + (cols - 1) + (subs - 1))

    def turned(pair):
        def make(k, piece):
            rows = rows_of(piece, width)
            return mm_paired(et_hi[k, rows, :], et_lo[k, rows, :], pair)

        return make

    @pl.when(row == 0)
    def _():
        first = to_pair(y_low, y_first, 0)
        first.start()
        get_c.wait()
        get_s.wait()
        make_spread()
        mapped_snd[...] = mm(spread[...], y_low[...])
        second = to_pair(mapped_snd, mapped_rcv, 1)
        second.start()
        make_spread_turn()
        turn_inverse()
        to_pair(sep_low, sep_low, 2).wait_recv()
        y_keep[...] = y_keep[...] - mm(spread_turn[...], sep_low[...])
        to_pair(root_keep, root_keep, 3).wait_recv()
        root_out[...] = root_keep[...]
        to_pair(give, take, 4).wait_recv()
        pair = paired(y_keep[...] - take[...])
        own, copies = scatter(turned(pair), back_snd, back_rcv, 7)
        for piece in range(PIECES):
            x_out[0, rows_of(piece, width), :] = gathered(own, back_rcv, copies, piece)
        finish(copies + [first, second])

    @pl.when(row != 0)
    def _():
        to_pair(y_low, y_first, 0).wait_recv()
        low = y_first[...]
        own, sends_a = scatter(
            lambda k, piece: mm(m_turn[k, rows_of(piece, width), :], low), a_snd, a_rcv, 0
        )
        started = apply_inverse()
        sends_b = []
        for piece in range(PIECES):
            rows = rows_of(piece, width)
            a_all[col, rows, :] = gathered(own, a_rcv, sends_a, piece).astype(BF16)
            sends_b.append(share_out(a_all.at[col, rows], PIECES + piece))
        get_c.wait()
        get_s.wait()
        make_spread()
        value = started
        for d in arrival:
            k = other(d)
            if d > 0:
                for piece in range(PIECES):
                    sends_b[piece][order.index(d)].wait_recv()
            value = value - (mm(e_hi[k], a_all[k]) + mm(e_lo[k], a_all[k]))
        y_keep[...] = value
        own_low = value.astype(BF16)
        to_pair(mapped_snd, mapped_rcv, 1).wait_recv()

        def separator_rows(k, piece):
            rows = piece_of(k, piece, share)
            return mm(spread[rows, :], own_low) + mapped_rcv[rows, :]

        own, sends_c = scatter(separator_rows, s_snd, s_rcv, 2)
        get_r.wait()
        get_t.wait()
        r_hi[...], r_lo[...] = halves(r_raw[...])
        for first in range(0, separator, step):
            ends = slice(first, first + step)
            rt_hi[ends, :], rt_lo[ends, :] = halves(r_raw[:, ends].T)
        rounds = subs.bit_length() - 1
        sends_z = []

        def exchange(total, piece, level):
            rows = rows_of(piece, share)
            z_snd[level, rows, :] = total.astype(BF16)
            copy = pltpu.make_async_remote_copy(
                z_snd.at[level, rows],
                z_rcv.at[level, rows],
                z_ssem.at[piece, level],
                z_rsem.at[piece, level],
                device_id={"sub": partner(sub, 1 << level)},
            )
            copy.start()
            sends_z.append(copy)
            return copy

        def received(total, copy, piece, level):
            copy.wait_recv()
            return total + z_rcv[level, rows_of(piece, share), :].astype(F32)

        flying = []
        for piece in range(PIECES):
            own[piece] = gathered(own, s_rcv, sends_c, piece)
            if rounds:
                flying.append(exchange(own[piece], piece, 0))
        make_spread_turn()
        for level in range(rounds):
            for piece in range(PIECES):
                own[piece] = received(own[piece], flying[piece], piece, level)
                if level + 1 < rounds:
                    flying[piece] = exchange(own[piece], piece, level + 1)
            if level == 0:
                turn_inverse()
        sends_d = []
        for piece in range(PIECES):
            rows = rows_of(piece, share)
            total = own[piece]
            high, low = halves(root_right[rows, :] - total)
            place = piece_of(col, piece, share)
            rhs_hi[place, :] = high
            rhs_lo[place, :] = low
            sends_d.append(share_out(rhs_hi.at[place], 3 * PIECES + piece))
        rest = share_out(rhs_lo.at[part(col, share)], 4 * PIECES)
        for sent in sends_d:
            for copy in sent:
                copy.wait_recv()
        half = mm(r_hi[...], rhs_hi[...]) + mm(r_lo[...], rhs_hi[...])
        for copy in rest:
            copy.wait_recv()
        pair_r = paired(half + mm(r_hi[...], rhs_lo[...]))

        def root_rows(k, piece):
            rows = piece_of(k, piece, share)
            return mm_paired(rt_hi[rows, :], rt_lo[rows, :], pair_r)

        own, sends_e = scatter(root_rows, t_snd, t_rcv, 5)
        sends_f = []
        for piece in range(PIECES):
            total = gathered(own, t_rcv, sends_e, piece)
            place = piece_of(col, piece, share)
            sep_low[place, :] = total.astype(BF16)
            sends_f.append(share_out(sep_low.at[place], 6 * PIECES + piece))
            root_out[rows_of(piece, share), :] = total
            root_keep[rows_of(piece, share), :] = total
        third = to_pair(root_keep, root_keep, 3)
        third.start()
        for sent in sends_f:
            for copy in sent:
                copy.wait_recv()
        fourth = to_pair(sep_low, sep_low, 2)
        fourth.start()
        pair = paired(y_keep[...] - mm(spread_turn[...], sep_low[...]))
        own, sends_g = scatter(turned(pair), back_snd, back_rcv, 7)
        sends_h = []
        for piece in range(PIECES):
            rows = rows_of(piece, width)
            total = gathered(own, back_rcv, sends_g, piece)
            x_all[col, rows, :] = total.astype(BF16)
            sends_h.append(share_out(x_all.at[col, rows], 8 * PIECES + piece))
            x_out[0, rows, :] = total
        total = jnp.zeros(give.shape, F32)
        for d in arrival:
            k = other(d)
            if d > 0:
                for piece in range(PIECES):
                    sends_h[piece][order.index(d)].wait_recv()
            total = total + mm(m_mask[k], x_all[k])
        give[...] = total
        fifth = to_pair(give, take, 4)
        fifth.start()
        finish([sends_a, sends_b, sends_c, sends_z, sends_d, rest, sends_e, sends_f])
        finish([sends_g, sends_h, third, fourth, fifth])


def write_out(x_ref, root_ref, x_out, root_out):
    x_out[...] = x_ref[...]
    root_out[...] = root_ref[...]


def shards(
    sizes,
    factor_cols,
    block_pattern,
    diag_inverse,
    coupling_cols,
    separator_rows,
    root_inverse,
    right_side,
    root_right,
):
    subs, cols = sizes
    width, panel = diag_inverse.shape[1:]
    share, separator = root_inverse.shape
    sources = right_side.shape[2]
    coupled = coupling_cols.shape[3]
    hbm = pl.BlockSpec(memory_space=pl.ANY)
    vmem = pl.BlockSpec(memory_space=pltpu.VMEM)
    V = pltpu.VMEM
    tile = (cols, width, width)
    scratch = [
        pltpu.SMEM(block_pattern.shape, jnp.int32),
        V(separator_rows.shape, jnp.int32),
        V(root_right.shape, F32),
        V((width, panel), F32),
        V((width, panel), BF16),
        V((width, coupled), BF16),
        V((share, separator), F32),
        V((panel, sources), F32),
        V(tile, BF16),
        V(tile, BF16),
        V(tile, BF16),
        V(tile, BF16),
        V(tile, BF16),
        V(tile, BF16),
        V((separator, width), BF16),
        V((width, separator), BF16),
        V((share, separator), BF16),
        V((share, separator), BF16),
        V((separator, share), BF16),
        V((separator, share), BF16),
        V((width, sources), F32),
        V((width, sources), BF16),
        V((width, sources), BF16),
        V((separator, sources), F32),
        V((separator, sources), F32),
        V((cols, width, sources), BF16),
        V((cols, width, sources), BF16),
        V((cols, width, sources), BF16),
        V((cols, share, sources), BF16),
        V((cols, share, sources), BF16),
        V((subs, share, sources), BF16),
        V((subs, share, sources), BF16),
        V((separator, sources), BF16),
        V((separator, sources), BF16),
        V((cols, share, sources), BF16),
        V((cols, share, sources), BF16),
        V((separator, sources), BF16),
        V((share, sources), F32),
        V((cols, width, sources), BF16),
        V((cols, width, sources), BF16),
        V((cols, width, sources), BF16),
        V((width, sources), F32),
        V((width, sources), F32),
        pltpu.SemaphoreType.DMA((7 + cols,)),
        pltpu.SemaphoreType.DMA((5,)),
        pltpu.SemaphoreType.DMA((5,)),
        pltpu.SemaphoreType.DMA((10 * PIECES, cols)),
        pltpu.SemaphoreType.DMA((10 * PIECES, cols)),
        pltpu.SemaphoreType.DMA((PIECES, subs)),
        pltpu.SemaphoreType.DMA((PIECES, subs)),
    ]
    solved = pl.pallas_call(
        functools.partial(kernel, sizes),
        out_shape=(
            jax.ShapeDtypeStruct((1, width, sources), F32),
            jax.ShapeDtypeStruct((share, sources), F32),
        ),
        in_specs=[hbm] * 8,
        out_specs=(vmem, vmem),
        scratch_shapes=scratch,
        compiler_params=pltpu.CompilerParams(
            collective_id=0, has_side_effects=True, vmem_limit_bytes=60 * 1024 * 1024
        ),
        name="tree_solve",
    )(
        factor_cols,
        block_pattern,
        diag_inverse,
        coupling_cols,
        separator_rows,
        root_inverse,
        right_side,
        root_right,
    )
    return pl.pallas_call(
        write_out,
        out_shape=tuple(jax.ShapeDtypeStruct(a.shape, a.dtype) for a in solved),
        in_specs=[vmem, vmem],
        out_specs=(vmem, vmem),
        name="write_out",
    )(*solved)


def solution(mesh):
    sizes = (mesh.shape["sub"], mesh.shape["col"])
    return jax.shard_map(
        functools.partial(shards, sizes),
        mesh=mesh,
        in_specs=(
            P("sub", None, "col", "row"),
            P("sub", None, None),
            P("sub", ("row", "col"), None),
            P("sub", "row", "col", None),
            P("sub", None),
            P("col", None),
            P("sub", "row", None),
            P("col", None),
        ),
        out_specs=(P("sub", ("row", "col"), None), P("col", None)),
        check_vma=False,
    )
```
